32 devices in a mesh: seq: 8 (over z, core), exp: 4 (over y, x).
Axes of the slice: x: 2, y: 2, z: 4, core: 2. Of those that a mesh axis runs over, the one named last changes fastest.
Arguments:
- layer_input: bfloat16 [4096, 1024], P(('seq', 'exp')), may hold values from -6 to 6
- layer_cotangent: bfloat16 [4096, 1024], P(('seq', 'exp')), may hold values from -6 to 6
- query_heads: bfloat16 [4096, 1024], P('seq', 'exp'), may hold values from -6 to 6
- key_heads: bfloat16 [4096, 1024], P('seq', 'exp'), may hold values from -6 to 6
- value_heads: bfloat16 [4096, 1024], P('seq', 'exp'), may hold values from -6 to 6
- key_grad_acc: float32 [4096, 1024], P('seq', 'exp'), may hold values from -0.6 to 0.6
- value_grad_acc: float32 [4096, 1024], P('seq', 'exp'), may hold values from -0.6 to 0.6
- out_proj: bfloat16 [1024, 1024], replicated, may hold values from -0.1875 to 0.1875
- router_proj: bfloat16 [1024, 4], replicated, may hold values from -0.1875 to 0.1875
- gate_proj: bfloat16 [4, 1024, 512], P('exp'), may hold values from -0.1875 to 0.1875
- up_proj: bfloat16 [4, 1024, 512], P('exp'), may hold values from -0.1875 to 0.1875
- down_proj: bfloat16 [4, 512, 1024], P('exp'), may hold values from -0.25 to 0.25
- expert_ids: int32 [4096, 2], P(('seq', 'exp')), may hold values from 0 to 3, all different within a row; in each aligned block of 128 rows (0 to 127, 128 to 255, ...) at most 96 rows name the same one
Outputs:
- input_grad: bfloat16 [4096, 1024], P(('seq', 'exp'))
- query_grad: bfloat16 [4096, 1024], P('seq', 'exp')
- key_grad: float32 [4096, 1024], P('seq', 'exp')
- value_grad: float32 [4096, 1024], P('seq', 'exp')
The draws below stay inside these ranges and needn't reach their ends.
Inputs may be any that keep to these rules, and one draw needn't show every extreme that they name: `expert_ids`: each row names two different experts; among the 128 rows of one device no expert is named by more than 96 rows, and in some devices' rows one expert is named by exactly 96.
All inputs are finite; a program needn't handle non-finite values.
Results may differ from the reference program's by a relative error of at most 0.023.
Values may be sent and summed in bfloat16 or wider, within the bound.
No kernel may reach another device: no remote copies, remote signals or barrier semaphores. Data moves between devices by JAX's collectives and lax.ppermute only.
A program may use at most 128 MiB of HBM per device.

```python
import math
import jax
import jax.numpy as jnp
import numpy as np
from jax import lax

D = 1024
H = 16
HEAD = 64
F = 512
TOK_DEV = 128
EXPERTS = 4
CAP = 96
ROWS = 512
LENGTH = 4096
N_SEQ = 8
N_EXP = 4


def drawn_values(key, salt):
    values = 1.4 * jax.random.normal(jax.random.fold_in(key, salt), (LENGTH, H * HEAD), jnp.float32)
    return jnp.clip(values, -6.0, 6.0)


def draw_query_heads(key, part):
    values = drawn_values(key, 11)
    return values.astype(jnp.bfloat16)


def draw_key_heads(key, part):
    values = drawn_values(key, 23)
    return values.astype(jnp.bfloat16)


def levels(rng, shape, shards, least, high):
    factor_of = 1.0
    for dim, parts in shards:
        steps = jax.random.uniform(jax.random.fold_in(jax.random.fold_in(rng, 6), dim), (parts,), jnp.float32, least / len(shards), high / len(shards))
        factor_of = factor_of * jnp.repeat(jnp.exp(steps), shape[dim] // parts).reshape((-1,) + (1,) * (len(shape) - 1 - dim))
    return factor_of


def shared_out(own_key, own, number, rows, amount, top, limit, skew):
    sequence = jax.random.permutation(own_key, amount)
    heavy_load, usual = portions_of(amount, rows * top, limit, skew, True), portions_of(amount, rows * top, limit, skew, False)
    places = jnp.arange(amount)

    def named(sizes, turn):
        used = int((sizes > 0).sum())
        fixed = max(1, used // 4)
        passed = fixed + (places - fixed + turn * (used - fixed)) % max(1, amount - fixed)
        return jnp.zeros((amount,), jnp.int32).at[sequence[jnp.where(places < fixed, places, passed)]].set(jnp.asarray(sizes, jnp.int32))

    sizes = jnp.where(number % 4 == 0, named(heavy_load, number // 4), named(usual, number - number // 4 - 1))
    mixed = jax.random.permutation(jax.random.fold_in(own, 3), amount)
    donor, sink = mixed[0:amount // 2 * 2:2], mixed[1:amount // 2 * 2:2]
    slack = jnp.minimum(sizes[donor] - 1, limit - sizes[sink]) // 2
    slack = jnp.where((donor == sequence[0]) | (sink == sequence[0]) | (sizes[sink] == 0), 0, jnp.maximum(slack, 0))
    passed = jax.random.randint(jax.random.fold_in(own, 4), (amount // 2,), 0, 1 << 20) % (slack + 1)
    sizes = sizes.at[donor].add(-passed).at[sink].add(passed)
    items = jnp.searchsorted(jnp.cumsum(sizes), jnp.arange(rows * top), side="right").astype(jnp.int32)
    listing = items.reshape(top, rows).T
    listing = listing[jax.random.permutation(jax.random.fold_in(own, 1), rows)]
    turn = jax.random.randint(jax.random.fold_in(own, 2), (rows, 1), 0, top)
    return jnp.take_along_axis(listing, (jnp.arange(top)[None, :] + turn) % top, axis=1)


def portions_of(amount, total, reach, lean, full):
    weights = [(1 << 20) // math.isqrt(rank ** lean) + 1 for rank in range(1, amount + 1)]
    largest = reach if full else min(reach, max(-(-total // amount), total * weights[0] // sum(weights)))
    least = 1 if total - largest >= amount - 1 else 0
    counts, spare = [largest] + [least] * (amount - 1), total - largest - least * (amount - 1)
    while spare > 0:
        candidates = [i for i in range(1, amount) if counts[i] < largest] or [i for i in range(1, amount) if counts[i] < reach]
        mass, left = sum([weights[i] for i in candidates]), spare
        for i in candidates:
            extra = min(reach - counts[i], max(1, left * weights[i] // mass), spare)
            counts[i] = counts[i] + extra
            spare = spare - extra
    return np.array(counts)


def bell_draw(key, extent, scale, limit, cuts=(), kind=jnp.bfloat16):
    gain = levels(key, extent, cuts, -0.22, 0.18) if cuts else 1.0
    values = jax.random.normal(key, extent, jnp.float32) * scale * gain
    return jnp.minimum(jnp.maximum(values, -limit), limit).astype(kind)


def setup_inputs(seed: int = 0) -> dict:
    keys = jax.random.split(jax.random.key(seed), 14)
    layer_input = bell_draw(keys[0], (LENGTH, D), 1.0, 6.0, ((0, 32),))
    layer_cotangent = bell_draw(keys[1], (LENGTH, D), 1.0, 6.0, ((0, 32),))
    query_heads = draw_query_heads(jax.random.fold_in(keys[13], 71), 0)
    key_heads = draw_key_heads(jax.random.fold_in(keys[13], 71), 0)
    value_heads = bell_draw(keys[4], (LENGTH, H * HEAD), 1.0, 6.0, ((0, 8), (1, 4)))
    key_grad_acc = bell_draw(keys[5], (LENGTH, H * HEAD), 0.1, 0.6, ((0, 8), (1, 4)), jnp.float32)
    value_grad_acc = bell_draw(keys[6], (LENGTH, H * HEAD), 0.1, 0.6, ((0, 8), (1, 4)), jnp.float32)
    out_proj = bell_draw(keys[7], (H * HEAD, D), (H * HEAD) ** -0.5, 0.1875)
    router_proj = bell_draw(keys[8], (D, EXPERTS), D ** -0.5, 0.1875)
    gate_proj = bell_draw(keys[9], (EXPERTS, D, F), D ** -0.5, 0.1875, ((0, 4),))
    up_proj = bell_draw(keys[10], (EXPERTS, D, F), D ** -0.5, 0.1875, ((0, 4),))
    down_proj = bell_draw(keys[11], (EXPERTS, F, D), F ** -0.5, 0.25, ((0, 4),))
    expert_ids_keys = jax.random.split(jax.random.fold_in(keys[12], 1), LENGTH // TOK_DEV)
    expert_ids_turns = jax.random.permutation(jax.random.fold_in(keys[12], 3), LENGTH // TOK_DEV)
    expert_ids = jax.vmap(lambda own, number: shared_out(jax.random.fold_in(keys[12], 2), own, number, TOK_DEV, EXPERTS, 2, CAP, 1))(expert_ids_keys, expert_ids_turns).reshape((LENGTH, 2))
    return {"layer_input": layer_input, "layer_cotangent": layer_cotangent, "query_heads": query_heads, "key_heads": key_heads, "value_heads": value_heads, "key_grad_acc": key_grad_acc, "value_grad_acc": value_grad_acc, "out_proj": out_proj, "router_proj": router_proj, "gate_proj": gate_proj, "up_proj": up_proj, "down_proj": down_proj, "expert_ids": expert_ids}


EPSILON = 1e-06

def normalize(block_rows):
    widened = block_rows.astype(jnp.float32)
    inverse = lax.rsqrt(lax.optimization_barrier(jnp.mean(widened * widened, axis=-1, keepdims=True)) + EPSILON)
    return (widened * inverse, inverse)

def norm_back(normed, inverse, upstream):
    row_inner = lax.optimization_barrier(jnp.mean(upstream * normed, axis=-1, keepdims=True))
    return (upstream - normed * row_inner) * inverse

def slot_matrix(choice_ids, expert_count, capacity):
    flat_ids = choice_ids.reshape(-1)
    member = (flat_ids[:, None] == jnp.arange(expert_count, dtype=jnp.int32)[None, :]).astype(jnp.int32)
    earlier = jnp.cumsum(member, axis=0) - member
    position = lax.optimization_barrier(jnp.sum(earlier * member, axis=1))
    slot_index = flat_ids * capacity + position
    slot_table = slot_index[None, :] == jnp.arange(expert_count * capacity, dtype=jnp.int32)[:, None]
    return slot_table.astype(jnp.bfloat16)

def expert_pass(inputs, cot_slots, gate_proj, up_proj, down_proj):
    highest = lax.Precision.HIGHEST
    wide_in = inputs.astype(jnp.float32)
    pre_gate = jnp.einsum('sjcd,jdf->sjcf', wide_in, gate_proj.astype(jnp.float32), precision=highest)
    pre_up = jnp.einsum('sjcd,jdf->sjcf', wide_in, up_proj.astype(jnp.float32), precision=highest)
    squashed = jax.nn.sigmoid(pre_gate)
    silu_gate = pre_gate * squashed
    hidden = (silu_gate * pre_up).astype(jnp.bfloat16)
    output = jnp.einsum('sjcf,jfd->sjcd', hidden.astype(jnp.float32), down_proj.astype(jnp.float32), precision=highest).astype(jnp.bfloat16)
    dhidden = jnp.einsum('sjcd,jfd->sjcf', cot_slots.astype(jnp.float32), down_proj.astype(jnp.float32), precision=highest)
    dgate_part = (dhidden * pre_up * squashed * (1.0 + pre_gate * (1.0 - squashed))).astype(jnp.bfloat16)
    dup_part = (dhidden * silu_gate).astype(jnp.bfloat16)
    dinput = jnp.einsum('sjcf,jdf->sjcd', dgate_part.astype(jnp.float32), gate_proj.astype(jnp.float32), precision=highest)
    dinput = dinput + jnp.einsum('sjcf,jdf->sjcd', dup_part.astype(jnp.float32), up_proj.astype(jnp.float32), precision=highest)
    return (output, dinput.astype(jnp.bfloat16))

def slab_backward(queries, key_slab, value_slab, grad_rows, has_prev, head_size):
    highest = lax.Precision.HIGHEST
    row_count, feature_width = queries.shape
    head_count = feature_width // head_size
    block_size = math.gcd(row_count, 512)
    query_split = queries.reshape(row_count, head_count, head_size).astype(jnp.float32)
    key_split = key_slab.reshape(2 * row_count, head_count, head_size).astype(jnp.float32)
    value_split = value_slab.reshape(2 * row_count, head_count, head_size).astype(jnp.float32)
    grad_split = grad_rows.reshape(row_count, head_count, head_size).astype(jnp.float32)
    key_pos = jnp.arange(2 * row_count, dtype=jnp.int32) - row_count
    key_live = (key_pos >= 0) | has_prev
    score_scale = 1.0 / math.sqrt(head_size)

    def one_block(running, block_start):
        key_sum, value_sum = running
        query_blk = lax.dynamic_slice_in_dim(query_split, block_start, block_size, 0)
        grad_blk = lax.dynamic_slice_in_dim(grad_split, block_start, block_size, 0)
        query_pos = block_start + jnp.arange(block_size, dtype=jnp.int32)
        allowed = (key_pos[None, :] <= query_pos[:, None]) & key_live[None, :]
        scores = jnp.einsum('qhe,khe->hqk', query_blk, key_split, precision=highest) * score_scale
        scores = jnp.where(allowed[None], scores, -jnp.inf)
        row_top = lax.optimization_barrier(jnp.max(scores, axis=-1, keepdims=True))
        row_total = lax.optimization_barrier(jnp.sum(jnp.exp(scores - row_top), axis=-1, keepdims=True))
        probs_full = jnp.exp(scores - (row_top + jnp.log(row_total)))
        dprobs = jnp.einsum('qhe,khe->hqk', grad_blk, value_split, precision=highest)
        row_inner = lax.optimization_barrier(jnp.sum(probs_full * dprobs, axis=-1, keepdims=True))
        dscores = (probs_full * (dprobs - row_inner) * score_scale).astype(jnp.bfloat16).astype(jnp.float32)
        probs_low = probs_full.astype(jnp.bfloat16).astype(jnp.float32)
        query_part = jnp.einsum('hqk,khe->qhe', dscores, key_split, precision=highest).astype(jnp.bfloat16)
        key_sum = key_sum + jnp.einsum('hqk,qhe->khe', dscores, query_blk, precision=highest)
        value_sum = value_sum + jnp.einsum('hqk,qhe->khe', probs_low, grad_blk, precision=highest)
        return ((key_sum, value_sum), query_part)
    starts = jnp.arange(row_count // block_size, dtype=jnp.int32) * block_size
    empty = jnp.zeros((2 * row_count, head_count, head_size), jnp.float32)
    (key_sum, value_sum), query_parts = lax.scan(one_block, (empty, empty), starts)
    return (query_parts.reshape(row_count, feature_width), key_sum.reshape(2 * row_count, feature_width), value_sum.reshape(2 * row_count, feature_width))

def reference(layer_input, layer_cotangent, query_heads, key_heads, value_heads, key_grad_acc, value_grad_acc, out_proj, router_proj, gate_proj, up_proj, down_proj, expert_ids):
    highest = lax.Precision.HIGHEST
    block_count = N_SEQ * N_EXP

    def moe_block(pieces):
        block_rows, cot_rows, block_ids = pieces
        normed, inverse = normalize(block_rows)
        routed = normed.astype(jnp.bfloat16)
        logits = jnp.dot(routed, router_proj, preferred_element_type=jnp.float32)
        member = block_ids[:, :, None] == jnp.arange(EXPERTS, dtype=jnp.int32)[None, None, :]
        chosen = lax.optimization_barrier(jnp.sum(jnp.where(member, logits[:, None, :], 0.0), axis=-1))
        gate_value = jax.nn.sigmoid(chosen).astype(jnp.bfloat16)
        gate_wide = gate_value.astype(jnp.float32)
        slot_table = slot_matrix(block_ids, EXPERTS, CAP)
        out_cot = (gate_wide[:, :, None] * cot_rows.astype(jnp.float32)[:, None, :]).astype(jnp.bfloat16)
        out_cot = out_cot.reshape(2 * TOK_DEV, D)
        routed_buf = jnp.dot(slot_table, jnp.repeat(routed, 2, axis=0), preferred_element_type=jnp.float32)
        routed_buf = routed_buf.astype(jnp.bfloat16).reshape(1, EXPERTS, CAP, D)
        cot_buf = jnp.dot(slot_table, out_cot, preferred_element_type=jnp.float32)
        cot_buf = cot_buf.astype(jnp.bfloat16).reshape(1, EXPERTS, CAP, D)
        output, dinput = expert_pass(routed_buf, cot_buf, gate_proj, up_proj, down_proj)
        back_out = jnp.dot(slot_table.T, output.reshape(EXPERTS * CAP, D), preferred_element_type=jnp.float32)
        back_in = jnp.dot(slot_table.T, dinput.reshape(EXPERTS * CAP, D), preferred_element_type=jnp.float32)
        cot_pairs = jnp.repeat(cot_rows, 2, axis=0).astype(jnp.float32)
        gate_dot = lax.optimization_barrier(jnp.sum(cot_pairs * back_out, axis=-1)).astype(jnp.bfloat16).reshape(TOK_DEV, 2)
        dlogit = gate_dot.astype(jnp.float32) * gate_wide * (1.0 - gate_wide)
        spread = lax.optimization_barrier(jnp.sum(jnp.where(member, dlogit[:, :, None], 0.0), axis=1))
        router_term = jnp.dot(spread, router_proj.astype(jnp.float32).T, precision=highest)
        dnormed = lax.optimization_barrier(jnp.sum(back_in.reshape(TOK_DEV, 2, D), axis=1)) + router_term
        return (cot_rows.astype(jnp.float32) + norm_back(normed, inverse, dnormed)).astype(jnp.bfloat16)
    input_grad = lax.map(moe_block, (layer_input.reshape(block_count, TOK_DEV, D), layer_cotangent.reshape(block_count, TOK_DEV, D), expert_ids.reshape(block_count, TOK_DEV, 2)))
    input_grad = input_grad.reshape(LENGTH, D)
    head_cot = jnp.dot(input_grad, out_proj.T, preferred_element_type=jnp.float32).astype(jnp.bfloat16)
    feature_width = H * HEAD
    zero_rows = jnp.zeros((ROWS, feature_width), key_heads.dtype)
    key_padded = jnp.concatenate([zero_rows, key_heads], axis=0)
    value_padded = jnp.concatenate([zero_rows, value_heads], axis=0)

    def slab_rows(row_index):
        first_row = (row_index * ROWS).astype(jnp.int32)
        queries = lax.dynamic_slice_in_dim(query_heads, first_row, ROWS, 0)
        grad_rows = lax.dynamic_slice_in_dim(head_cot, first_row, ROWS, 0)
        key_slab = lax.dynamic_slice_in_dim(key_padded, first_row, 2 * ROWS, 0)
        value_slab = lax.dynamic_slice_in_dim(value_padded, first_row, 2 * ROWS, 0)
        return slab_backward(queries, key_slab, value_slab, grad_rows, row_index > 0, HEAD)
    query_grad, key_all, value_all = lax.map(slab_rows, jnp.arange(N_SEQ, dtype=jnp.int32))
    query_grad = query_grad.reshape(LENGTH, feature_width)
    zero_tail = jnp.zeros((1, ROWS, feature_width), jnp.float32)
    key_part = key_all[:, ROWS:] + jnp.concatenate([key_all[1:, :ROWS], zero_tail], axis=0)
    value_part = value_all[:, ROWS:] + jnp.concatenate([value_all[1:, :ROWS], zero_tail], axis=0)
    key_grad = key_grad_acc + key_part.reshape(LENGTH, feature_width)
    value_grad = value_grad_acc + value_part.reshape(LENGTH, feature_width)
    return (input_grad, query_grad, key_grad, value_grad)
```

```python
import functools
import math

import jax
import jax.numpy as jnp
from jax import lax
from jax.experimental import pallas as pl
from jax.experimental.pallas import tpu as pltpu
from jax.sharding import PartitionSpec as P

HEAD = 64
EPSILON = 1e-06
F32 = jnp.float32
BF16 = jnp.bfloat16
NEG = -1e30
NN = (((1,), (0,)), ((), ()))
NT = (((1,), (1,)), ((), ()))
TN = (((0,), (0,)), ((), ()))


def dot(a, b, dims=NN):
    return lax.dot_general(a, b, dims, preferred_element_type=F32)


def vmem():
    return pl.BlockSpec(memory_space=pltpu.VMEM)


def smem():
    return pl.BlockSpec(memory_space=pltpu.SMEM)


def call(body, outs, operands, scalars=1, scratch=(), aliases=None, cost=None):
    return pl.pallas_call(
        body,
        out_shape=[jax.ShapeDtypeStruct(s, d) for s, d in outs],
        in_specs=[smem()] * scalars + [vmem()] * (len(operands) - scalars),
        out_specs=[vmem()] * len(outs),
        scratch_shapes=list(scratch),
        input_output_aliases=aliases or {},
        compiler_params=pltpu.CompilerParams(vmem_limit_bytes=60 * 1024 * 1024),
        cost_estimate=cost,
    )(*operands)


def slot_positions(me, ids_t, groups):
    tokens = ids_t.shape[1]
    rows = max(16, groups)
    expert = lax.broadcasted_iota(jnp.int32, (rows, tokens), 0) ^ me
    member = (ids_t[0:1, :] == expert) | (ids_t[1:2, :] == expert)
    before = lax.broadcasted_iota(jnp.int32, (tokens, tokens), 0) < lax.broadcasted_iota(
        jnp.int32, (tokens, tokens), 1
    )
    rank = dot(jnp.where(member, 1.0, 0.0).astype(BF16), jnp.where(before, 1.0, 0.0).astype(BF16))
    return jnp.where(member, rank, -1.0)


def slot_table(position, d, slots):
    tokens = position.shape[1]
    index = lax.broadcasted_iota(jnp.int32, (slots, tokens), 0).astype(F32)
    return jnp.where(position[d : d + 1, :] == index, 1.0, 0.0).astype(BF16)


def normalize(rows):
    wide = rows.astype(F32)
    inverse = lax.rsqrt(jnp.mean(wide * wide, axis=-1, keepdims=True) + EPSILON)
    return wide * inverse, inverse


def pack_body(groups, slots, me_ref, x_ref, cot_ref, ids_ref, *outs):
    position = slot_positions(me_ref[0], ids_ref[...], groups)
    routed = normalize(x_ref[...])[0].astype(BF16)
    cot = cot_ref[...]
    for d in range(groups):
        table = slot_table(position, d, slots)
        outs[d][:slots, :] = dot(table, routed).astype(BF16)
        outs[d][slots:, :] = dot(table, cot).astype(BF16)


def expert_body(me_ref, rows_ref, router_ref, gate_ref, up_ref, down_ref, out_ref):
    slots = out_ref.shape[0]
    rows = rows_ref[:slots, :]
    cot = rows_ref[slots:, :]
    router = router_ref[...]
    logits = dot(rows, router, NT)
    lane = lax.broadcasted_iota(jnp.int32, logits.shape, 1)
    logit = jnp.sum(jnp.where(lane == me_ref[0], logits, 0.0), axis=-1, keepdims=True)
    gate = jax.nn.sigmoid(logit).astype(BF16).astype(F32)
    row = lax.broadcasted_iota(jnp.int32, router.shape, 0)
    column = jnp.sum(
        jnp.where(row == me_ref[0], router.astype(F32), 0.0), axis=0, keepdims=True
    )
    gate_w = gate_ref[0]
    up_w = up_ref[0]
    pre_gate = dot(rows, gate_w)
    pre_up = dot(rows, up_w)
    back = dot(cot, down_ref[0], NT)
    squashed = jax.nn.sigmoid(pre_gate)
    silu = pre_gate * squashed
    hidden = (silu * pre_up).astype(BF16).astype(F32)
    gate_dot = jnp.sum(hidden * back, axis=-1, keepdims=True).astype(BF16).astype(F32)
    dhidden = gate * back
    dgate = (dhidden * pre_up * squashed * (1.0 + pre_gate * (1.0 - squashed))).astype(BF16)
    dup = (dhidden * silu).astype(BF16)
    dinput = dot(dgate, gate_w, NT) + dot(dup, up_w, NT)
    dlogit = gate_dot * gate * (1.0 - gate)
    out_ref[...] = (dinput + dlogit * column).astype(BF16)


def return_body(groups, slots, me_ref, x_ref, cot_ref, ids_ref, proj_ref, *refs):
    back = refs[:groups]
    grad_ref = refs[groups]
    heads = refs[groups + 1 :]
    position = slot_positions(me_ref[0], ids_ref[...], groups)
    normed, inverse = normalize(x_ref[...])
    upstream = jnp.zeros(normed.shape, F32)
    for d in range(groups):
        upstream = upstream + dot(slot_table(position, d, slots), back[d][...], TN)
    inner = jnp.mean(upstream * normed, axis=-1, keepdims=True)
    grad = (cot_ref[...].astype(F32) + (upstream - normed * inner) * inverse).astype(BF16)
    grad_ref[...] = grad
    width = heads[0].shape[1]
    for d in range(groups):
        first = pl.multiple_of((me_ref[0] ^ d) * width, width)
        heads[d][...] = dot(grad, proj_ref[pl.ds(first, width), :], NT).astype(BF16)


def head_lanes(rows, head):
    if rows.shape[1] == HEAD:
        return rows
    lane = lax.broadcasted_iota(jnp.int32, rows.shape, 1)
    return jnp.where((lane >= head * HEAD) & (lane < (head + 1) * HEAD), rows, jnp.zeros_like(rows))


def causal(tile):
    return lax.broadcasted_iota(jnp.int32, (tile, tile), 0) <= lax.broadcasted_iota(
        jnp.int32, (tile, tile), 1
    )


EXP_SCALE = math.log2(math.e) / math.sqrt(HEAD)


def probs_body(
    tile, prev_ref, q_ref, kp_ref, k_ref, vp_ref, v_ref, probs_ref, stats_ref, kt_ref, s_ref
):
    rows, width = q_ref.shape
    heads = width // HEAD
    live = prev_ref[0] > 0
    keys_prev = kp_ref[...]
    keys_own = k_ref[...]
    kt_ref[:, :rows] = keys_prev.astype(F32).T.astype(BF16)
    kt_ref[:, rows:] = keys_own.astype(F32).T.astype(BF16)
    vt_prev = vp_ref[...].astype(F32).T.astype(BF16)
    vt_own = v_ref[...].astype(F32).T.astype(BF16)
    allowed = causal(tile)
    for head in range(heads):
        lanes = slice(head * HEAD, (head + 1) * HEAD)
        for first in range(0, rows, tile):
            own = first + tile
            query = head_lanes(q_ref[first:own, :], head)
            s_prev = dot(keys_prev, query, NT)
            s_prev = jnp.where(live, s_prev, NEG)
            s_ref[:rows, :] = s_prev
            top = jnp.max(s_prev, axis=0, keepdims=True)
            if first:
                s_mid = dot(keys_own[:first], query, NT)
                s_ref[rows : rows + first, :] = s_mid
                top = jnp.maximum(top, jnp.max(s_mid, axis=0, keepdims=True))
            s_own = jnp.where(allowed, dot(keys_own[first:own], query, NT), NEG)
            s_ref[rows + first : rows + own, :] = s_own
            top = jnp.maximum(top, jnp.max(s_own, axis=0, keepdims=True)) * EXP_SCALE
            powers = jnp.exp2(s_ref[: rows + own, :] * EXP_SCALE - top)
            total = jnp.sum(powers, axis=0, keepdims=True)
            low = (powers * (1.0 / total)).astype(BF16)
            probs_ref[head, : rows + own, first:own] = low
            mixed = dot(vt_prev[lanes], low[:rows]) + dot(vt_own[lanes, :own], low[rows:])
            stats_ref[lanes, first:own] = mixed
            stats_ref[width + head : width + head + 1, first:own] = top + jnp.log2(total)
    stats_ref[width + heads :, :] = jnp.zeros((stats_ref.shape[0] - width - heads, rows), F32)


def next_probs_body(next_ref, q_ref, k_ref, stats_ref, probs_ref):
    rows, width = q_ref.shape
    live = next_ref[0] > 0
    keys = k_ref[...]
    for head in range(width // HEAD):
        scores = dot(keys, head_lanes(q_ref[...], head), NT)
        log_total = stats_ref[width + head : width + head + 1, :]
        exponent = jnp.where(live, scores * EXP_SCALE - log_total, NEG)
        probs_ref[head] = jnp.exp2(exponent).astype(BF16)


def own_body(
    groups,
    tile,
    me_ref,
    q_ref,
    vp_ref,
    v_ref,
    probs_ref,
    stats_ref,
    kt_ref,
    ka_ref,
    va_ref,
    *refs,
):
    arrived = refs[:groups]
    dq_ref, dk_ref, dv_ref, cot_ref, dqt_ref = refs[groups:]
    rows, width = q_ref.shape
    tokens = arrived[0].shape[0]
    scale = 1.0 / math.sqrt(HEAD)
    for d in range(groups):
        first = pl.multiple_of((me_ref[0] ^ d) * tokens, tokens)
        cot_ref[pl.ds(first, tokens), :] = arrived[d][...]
    values_prev = vp_ref[...]
    values_own = v_ref[...]
    dk_ref[...] = ka_ref[...]
    dv_ref[...] = va_ref[...]
    for first in range(0, rows, tile):
        own = first + tile
        cot_tile = cot_ref[first:own, :]
        product = cot_tile.astype(F32).T * stats_ref[:width, first:own]
        for head in range(width // HEAD):
            lanes = slice(head * HEAD, (head + 1) * HEAD)
            inner = jnp.sum(product[lanes], axis=0, keepdims=True) * scale
            cot = head_lanes(cot_tile, head)
            small = cot * BF16(scale)
            dp_prev = dot(values_prev, small, NT)
            dp_own = dot(values_own[:own], small, NT)
            low_prev = probs_ref[head, :rows, first:own]
            low_own = probs_ref[head, rows : rows + own, first:own]
            ds_prev = (low_prev.astype(F32) * (dp_prev - inner)).astype(BF16)
            ds_own = (low_own.astype(F32) * (dp_own - inner)).astype(BF16)
            dqt_ref[lanes, first:own] = dot(kt_ref[lanes, :rows], ds_prev) + dot(
                kt_ref[lanes, rows : rows + own], ds_own
            )
            dk_ref[:own, :] += dot(ds_own, head_lanes(q_ref[first:own, :], head))
            dv_ref[:own, :] += dot(low_own, cot)
    dq_ref[...] = dqt_ref[...].T.astype(BF16)


def next_body(groups, me_ref, q_ref, v_ref, probs_ref, stats_ref, dk_in, dv_in, cot_in, dk_ref, dv_ref, cot_ref):
    rows, width = q_ref.shape
    tokens = rows // groups
    scale = 1.0 / math.sqrt(HEAD)
    for d in range(groups):
        first = pl.multiple_of((me_ref[0] ^ d) * tokens, tokens)
        cot_ref[pl.ds(first, tokens), :] = cot_in[d * tokens : (d + 1) * tokens, :]
    values = v_ref[...]
    cot_all = cot_ref[...]
    product = cot_all.astype(F32).T * stats_ref[:width, :]
    dk = dk_in[...]
    dv = dv_in[...]
    for head in range(width // HEAD):
        lanes = slice(head * HEAD, (head + 1) * HEAD)
        inner = jnp.sum(product[lanes], axis=0, keepdims=True) * scale
        cot = head_lanes(cot_all, head)
        dp = dot(values, cot * BF16(scale), NT)
        low = probs_ref[head]
        ds = (low.astype(F32) * (dp - inner)).astype(BF16)
        dk = dk + dot(ds, head_lanes(q_ref[...], head))
        dv = dv + dot(low, cot)
    dk_ref[...] = dk
    dv_ref[...] = dv


def across(block, d):
    size = lax.axis_size("exp")
    return lax.ppermute(block, "exp", [(i, i ^ d) for i in range(size)])


def along(block, shift):
    size = lax.axis_size("seq")
    return lax.ppermute(block, "seq", [(i, (i + shift) % size) for i in range(size)])


def body(
    layer_input,
    layer_cotangent,
    query_heads,
    key_heads,
    value_heads,
    key_grad_acc,
    value_grad_acc,
    out_proj,
    router_proj,
    gate_proj,
    up_proj,
    down_proj,
    expert_ids,
):
    tokens, features = layer_input.shape
    rows, width = query_heads.shape
    heads = width // HEAD
    groups = lax.axis_size("exp")
    assert groups & (groups - 1) == 0 and gate_proj.shape[0] == 1
    experts = groups
    capacity = 3 * tokens // experts
    slots = -(-capacity // 16) * 16
    tile = math.gcd(rows, 256)
    me = lax.axis_index("exp").astype(jnp.int32).reshape(1)
    seq = lax.axis_index("seq")
    has_prev = (seq > 0).astype(jnp.int32).reshape(1)
    has_next = (seq < lax.axis_size("seq") - 1).astype(jnp.int32).reshape(1)
    ids_t = expert_ids.T
    router_t = router_proj.T

    packed = call(
        functools.partial(pack_body, groups, slots),
        [((2 * slots, features), BF16)] * groups,
        [me, layer_input, layer_cotangent, ids_t],
    )
    arrived = [packed[0]] + [across(packed[d], d) for d in range(1, groups)]

    key_prev = along(key_heads, 1)
    value_prev = along(value_heads, 1)
    query_next = along(query_heads, -1)

    def expert(block):
        return call(
            expert_body,
            [((slots, features), BF16)],
            [me, block, router_t, gate_proj, up_proj, down_proj],
        )[0]

    done = [expert(block) for block in arrived]
    back = [done[0]] + [across(done[d], d) for d in range(1, groups)]

    stat_rows = width + max(8, heads)
    probs, stats, keys_t = call(
        functools.partial(probs_body, tile),
        [
            ((heads, 2 * rows, rows), BF16),
            ((stat_rows, rows), F32),
            ((width, 2 * rows), BF16),
        ],
        [has_prev, query_heads, key_prev, key_heads, value_prev, value_heads],
        scratch=[pltpu.VMEM((2 * rows, tile), F32)],
    )
    stats_next = along(stats, -1)
    probs_next = call(
        next_probs_body,
        [((heads, rows, rows), BF16)],
        [has_next, query_next, key_heads, stats_next],
    )[0]

    returned = call(
        functools.partial(return_body, groups, slots),
        [((tokens, features), BF16)] + [((tokens, width), BF16)] * groups,
        [me, layer_input, layer_cotangent, ids_t, out_proj, *back],
    )
    input_grad, head_cot = returned[0], returned[1:]
    cot = [head_cot[0]] + [across(head_cot[d], d) for d in range(1, groups)]
    cot_next = along(jnp.concatenate(cot, axis=0), -1)

    query_grad, key_sum, value_sum = call(
        functools.partial(own_body, groups, tile),
        [((rows, width), BF16), ((rows, width), F32), ((rows, width), F32)],
        [
            me,
            query_heads,
            value_prev,
            value_heads,
            probs,
            stats,
            keys_t,
            key_grad_acc,
            value_grad_acc,
            *cot,
        ],
        scratch=[
            pltpu.VMEM((rows, width), BF16),
            pltpu.VMEM((width, rows), F32),
        ],
    )
    key_grad, value_grad = call(
        functools.partial(next_body, groups),
        [((rows, width), F32), ((rows, width), F32)],
        [me, query_next, value_heads, probs_next, stats_next, key_sum, value_sum, cot_next],
        scratch=[pltpu.VMEM((rows, width), BF16)],
    )
    return (input_grad, query_grad, key_grad, value_grad)


def solution(mesh):
    in_specs = (
        P(("seq", "exp"), None),
        P(("seq", "exp"), None),
        P("seq", "exp"),
        P("seq", "exp"),
        P("seq", "exp"),
        P("seq", "exp"),
        P("seq", "exp"),
        P(),
        P(),
        P("exp", None, None),
        P("exp", None, None),
        P("exp", None, None),
        P(("seq", "exp"), None),
    )
    out_specs = (P(("seq", "exp"), None), P("seq", "exp"), P("seq", "exp"), P("seq", "exp"))
    return jax.shard_map(body, mesh=mesh, in_specs=in_specs, out_specs=out_specs, check_vma=False)
```
